512 devices in a mesh: section: 2 (over z_hi), ctx: 32 (over z_lo, y), chan: 8 (over x, core).
Axes of the slice: x: 4, y: 4, z: 16 (z_hi: 2, z_lo: 8; z = z_hi * 8 + z_lo), core: 2. Of those that a mesh axis runs over, the one named last changes fastest.
Arguments:
- queries: bfloat16 [2, 8192, 8192], P('section', 'ctx', 'chan'), may hold values from -6 to 6
- keys: bfloat16 [2, 8192, 8192], P('section', 'ctx', 'chan'), may hold values from -6 to 6
- values: bfloat16 [8192, 8192], P('ctx', 'chan'), may hold values from -6 to 6
- cotangent: bfloat16 [8192, 8192], P('ctx', 'chan'), may hold values from -6 to 6
- short_filter: float32 [2, 3, 3, 8192], P('section', None, None, 'chan'), may hold values from -4 to 4
- mix_filter: bfloat16 [2, 128, 8192], P('section', None, 'chan'), may hold values from -0.5 to 0.5
- skip: float32 [2, 8192], P('section', 'chan'), may hold values from -5 to 5
Outputs:
- outputs: bfloat16 [2, 8192, 8192], P('section', 'ctx', 'chan')
- grad_q: bfloat16 [2, 8192, 8192], P('section', 'ctx', 'chan')
- grad_k: bfloat16 [2, 8192, 8192], P('section', 'ctx', 'chan')
- grad_input: bfloat16 [2, 8192, 8192], P('section', 'ctx', 'chan')
- grad_filter: float32 [2, 128, 8192], P('section', 'ctx', 'chan')
The draws below stay inside these ranges and needn't reach their ends.
All inputs are finite; a program needn't handle non-finite values.
Results may differ from the reference program's by a relative error of at most 0.015.
Values may be sent and summed in bfloat16 or wider, within the bound.
A program may use at most 64 MiB of HBM per device.

```python
from functools import partial
import jax
import jax.numpy as jnp
from jax import lax

D = 8192
TAPS = 128
TOKENS = 8192
SECTIONS = 2


def levels(rng, dims, split, low, largest):
    factor_of = 1.0
    for dim, shards_of in split:
        steps = jax.random.uniform(jax.random.fold_in(jax.random.fold_in(rng, 6), dim), (shards_of,), jnp.float32, low / len(split), largest / len(split))
        factor_of = factor_of * jnp.repeat(jnp.exp(steps), dims[dim] // shards_of).reshape((-1,) + (1,) * (len(dims) - 1 - dim))
    return factor_of


def normal_values(own_key, extent, spread, most, cuts=(), held_as=jnp.bfloat16):
    loudness = levels(own_key, extent, cuts, -0.22, 0.18) if cuts else 1.0
    values = jax.random.normal(own_key, extent, jnp.float32) * spread * loudness
    return jnp.minimum(jnp.maximum(values, -most), most).astype(held_as)


def setup_inputs(seed: int = 0) -> dict:
    key_of = jax.random.split(jax.random.key(seed), 8)
    return {
        "queries": normal_values(key_of[0], (SECTIONS, TOKENS, D), 1.0, 6.0, ((0, 2), (1, 32), (2, 8))),
        "keys": normal_values(key_of[1], (SECTIONS, TOKENS, D), 1.0, 6.0, ((0, 2), (1, 32), (2, 8))),
        "values": normal_values(key_of[2], (TOKENS, D), 1.0, 6.0, ((0, 32), (1, 8))),
        "cotangent": normal_values(key_of[3], (TOKENS, D), 1.0, 6.0, ((0, 32), (1, 8))),
        "short_filter": normal_values(key_of[4], (SECTIONS, 3, 3, D), 0.7, 4.0, ((0, 2), (3, 8)), jnp.float32),
        "mix_filter": normal_values(key_of[5], (SECTIONS, TAPS, D), TAPS ** -0.5, 0.5, ((0, 2), (2, 8))),
        "skip": normal_values(key_of[6], (SECTIONS, D), 1.0, 5.0, ((0, 2), (1, 8)), jnp.float32),
    }


def channel_blocks(func, arrays):
    total = arrays[0].shape[1]
    block = 1024 if total % 1024 == 0 else total
    groups = total // block
    stacked = tuple(jnp.transpose(item.reshape(item.shape[0], groups, block), (1, 0, 2)) for item in arrays)
    result = lax.map(lambda pieces: func(*pieces), stacked)
    return jnp.transpose(result, (1, 0, 2)).reshape(result.shape[1], total)


def causal_mix(signal, taps):
    length = signal.shape[0]
    spectrum = jnp.fft.rfft(signal, 2 * length, axis=0) * jnp.fft.rfft(taps, 2 * length, axis=0)
    return jnp.fft.irfft(spectrum, 2 * length, axis=0)[:length]


def future_mix(grads, taps):
    length = grads.shape[0]
    spectrum = jnp.fft.rfft(grads, 2 * length, axis=0) * jnp.conj(jnp.fft.rfft(taps, 2 * length, axis=0))
    return jnp.fft.irfft(spectrum, 2 * length, axis=0)[:length]


def lag_sums(grads, signal, reach):
    length = grads.shape[0]
    spectrum = jnp.fft.rfft(grads, 2 * length, axis=0) * jnp.conj(jnp.fft.rfft(signal, 2 * length, axis=0))
    return jnp.fft.irfft(spectrum, 2 * length, axis=0)[:reach]


def short_ref(rows, weights):
    widened = jnp.concatenate([jnp.zeros((2, rows.shape[1]), jnp.float32), rows.astype(jnp.float32)], axis=0)
    return weights[0] * widened[2:] + weights[1] * widened[1:-1] + weights[2] * widened[:-2]


def short_back(rows, weights):
    widened = jnp.concatenate([rows.astype(jnp.float32), jnp.zeros((2, rows.shape[1]), jnp.float32)], axis=0)
    return weights[0] * widened[:-2] + weights[1] * widened[1:-1] + weights[2] * widened[2:]


def forward(query_rows, key_rows, value_rows, short_taps, mix_taps, skip_row):
    q_short = short_ref(query_rows, short_taps[0])
    k_short = short_ref(key_rows, short_taps[1])
    v_short = short_ref(value_rows, short_taps[2])
    product = lax.optimization_barrier((k_short * v_short).astype(jnp.bfloat16))
    product_wide = product.astype(jnp.float32)
    mixed = channel_blocks(causal_mix, (product_wide, mix_taps.astype(jnp.float32))) + skip_row * product_wide
    output = (q_short * mixed).astype(jnp.bfloat16)
    return output, (q_short, mixed, product_wide, k_short, v_short)


def backward(grad_out, saved, short_taps, mix_taps, skip_row):
    q_short, mixed, product_wide, k_short, v_short = saved
    grad_wide = grad_out.astype(jnp.float32)
    grad_mix = lax.optimization_barrier((grad_wide * q_short).astype(jnp.bfloat16))
    grad_gate = (grad_wide * mixed).astype(jnp.bfloat16)
    mix_wide = grad_mix.astype(jnp.float32)
    grad_product = channel_blocks(future_mix, (mix_wide, mix_taps.astype(jnp.float32))) + skip_row * mix_wide
    grad_kshort = (grad_product * v_short).astype(jnp.bfloat16)
    grad_vshort = (grad_product * k_short).astype(jnp.bfloat16)
    grad_query = short_back(grad_gate, short_taps[0]).astype(jnp.bfloat16)
    grad_key = short_back(grad_kshort, short_taps[1]).astype(jnp.bfloat16)
    grad_value = short_back(grad_vshort, short_taps[2]).astype(jnp.bfloat16)
    taps_grad = channel_blocks(partial(lag_sums, reach=TAPS), (mix_wide, product_wide))
    return grad_query, grad_key, grad_value, taps_grad


def reference(queries, keys, values, cotangent, short_filter, mix_filter, skip):
    first_out, first_saved = forward(queries[0], keys[0], values, short_filter[0], mix_filter[0], skip[0])
    second_out, second_saved = forward(queries[1], keys[1], first_out, short_filter[1], mix_filter[1], skip[1])
    later = backward(cotangent, second_saved, short_filter[1], mix_filter[1], skip[1])
    earlier = backward(later[2], first_saved, short_filter[0], mix_filter[0], skip[0])
    outputs = jnp.stack([first_out, second_out])
    grad_q = jnp.stack([earlier[0], later[0]])
    grad_k = jnp.stack([earlier[1], later[1]])
    grad_input = jnp.stack([earlier[2], later[2]])
    grad_filter = jnp.stack([earlier[3], later[3]])
    return (outputs, grad_q, grad_k, grad_input, grad_filter)
```

```python
import jax
import jax.numpy as jnp
from jax import lax
from jax.sharding import PartitionSpec as P


def shifted(value, axis, by):
    peers = lax.axis_size(axis)
    pairs = [(i, i + by) for i in range(peers) if 0 <= i + by < peers]
    return lax.ppermute(value, axis, pairs)


def halving_scatter(part, axis):
    peers = lax.axis_size(axis)
    steps = peers.bit_length() - 1
    if peers != 1 << steps or part.shape[0] % peers:
        return lax.psum_scatter(part, axis, scatter_dimension=0, tiled=True)
    me = lax.axis_index(axis)
    rows = part.shape[0] // peers
    held = part.reshape((2,) * steps + (rows,) + part.shape[1:])
    remaining = [steps - 1 - k for k in range(steps)]
    order = sorted(range(steps), key=lambda b: (b % 2, b))
    for bit in order:
        at = remaining.index(bit)
        mine = (me >> bit) & 1
        keep = lax.dynamic_index_in_dim(held, mine, axis=at, keepdims=False)
        give = lax.dynamic_index_in_dim(held, 1 - mine, axis=at, keepdims=False)
        got = lax.ppermute(give, axis, [(i, i ^ (1 << bit)) for i in range(peers)])
        held = keep + got
        remaining.pop(at)
    return held.reshape((rows,) + part.shape[1:])


def depthwise(source, kernel):
    result = lax.conv_general_dilated(
        source[None],
        kernel[:, None, :],
        (1,),
        "VALID",
        dimension_numbers=("NWC", "WIO", "NWC"),
        feature_group_count=source.shape[1],
        preferred_element_type=jnp.float32,
    )
    return result[0]


def short_conv(padded, weights, rows_here):
    widened = padded.astype(jnp.float32)
    return (
        weights[0] * widened[2 : 2 + rows_here]
        + weights[1] * widened[1 : 1 + rows_here]
        + weights[2] * widened[0:rows_here]
    )


def short_back(padded, weights, rows_here):
    widened = padded.astype(jnp.float32)
    return (
        weights[0] * widened[0:rows_here]
        + weights[1] * widened[1 : 1 + rows_here]
        + weights[2] * widened[2 : 2 + rows_here]
    )


def forward(query_rows, key_rows, value_rows, short_taps, mix_taps, skip_row):
    extent = mix_taps.shape[0]
    rows_here = query_rows.shape[0]
    rim_q, rim_k, rim_v = shifted(
        (query_rows[-2:], key_rows[-(extent + 1) :], value_rows[-(extent + 1) :]), "ctx", 1
    )
    q_ext = jnp.concatenate([rim_q, query_rows], axis=0)
    k_big = jnp.concatenate([rim_k, key_rows], axis=0)
    v_big = jnp.concatenate([rim_v, value_rows], axis=0)
    k_big_short = short_conv(k_big, short_taps[1], rows_here + extent - 1)
    v_big_short = short_conv(v_big, short_taps[2], rows_here + extent - 1)
    product_ext = lax.optimization_barrier((k_big_short * v_big_short).astype(jnp.bfloat16))
    k_short = k_big_short[extent - 1 :]
    v_short = v_big_short[extent - 1 :]
    k_ext = k_big[extent - 1 :]
    v_ext = v_big[extent - 1 :]
    q_short = short_conv(q_ext, short_taps[0], rows_here)
    product_here = product_ext[extent - 1 :]
    mixed = depthwise(product_ext, mix_taps[::-1]) + skip_row * product_here.astype(jnp.float32)
    output = (q_short * mixed).astype(jnp.bfloat16)
    return (output, (q_short, mixed, product_ext, k_short, v_short, k_ext, v_ext))


def backward(grad_out, saved, short_taps, mix_taps, skip_row):
    q_short, mixed, product_ext, k_short, v_short, k_ext, v_ext = saved
    extent = mix_taps.shape[0]
    rows_here = q_short.shape[0]
    grad_wide = grad_out.astype(jnp.float32)
    grad_mix = lax.optimization_barrier((grad_wide * q_short).astype(jnp.bfloat16))
    grad_gate = (grad_wide * mixed).astype(jnp.bfloat16)
    rim_mix, rim_gate, rim_k, rim_v = shifted(
        (grad_mix[: extent + 1], grad_gate[:2], k_ext[2:4], v_ext[2:4]), "ctx", -1
    )
    mix_big = jnp.concatenate([grad_mix, rim_mix], axis=0)
    grad_product = depthwise(mix_big, mix_taps) + skip_row * mix_big[: rows_here + 2].astype(
        jnp.float32
    )
    k_next = short_conv(jnp.concatenate([k_ext[-2:], rim_k], axis=0), short_taps[1], 2)
    v_next = short_conv(jnp.concatenate([v_ext[-2:], rim_v], axis=0), short_taps[2], 2)
    kgrad_ext = (grad_product * jnp.concatenate([v_short, v_next], axis=0)).astype(jnp.bfloat16)
    vgrad_ext = (grad_product * jnp.concatenate([k_short, k_next], axis=0)).astype(jnp.bfloat16)
    gate_ext = jnp.concatenate([grad_gate, rim_gate], axis=0)
    grad_query = short_back(gate_ext, short_taps[0], rows_here).astype(jnp.bfloat16)
    grad_key = short_back(kgrad_ext, short_taps[1], rows_here).astype(jnp.bfloat16)
    grad_value = short_back(vgrad_ext, short_taps[2], rows_here).astype(jnp.bfloat16)
    taps_part = depthwise(product_ext, grad_mix)[::-1]
    return (grad_query, grad_key, grad_value, taps_part)


def body(queries, keys, values, cotangent, short_filter, mix_filter, skip):
    section_index = lax.axis_index("section")
    leading = section_index == 0
    short_taps = short_filter[0]
    mix_taps = mix_filter[0]
    skip_row = skip[0]
    first_out, first_saved = forward(queries[0], keys[0], values, short_taps, mix_taps, skip_row)
    handed = shifted(first_out, "section", 1)
    second_out, second_saved = forward(queries[0], keys[0], handed, short_taps, mix_taps, skip_row)
    later = backward(cotangent, second_saved, short_taps, mix_taps, skip_row)
    returned = shifted(later[2], "section", -1)
    earlier = backward(returned, first_saved, short_taps, mix_taps, skip_row)

    def select(upper, lower):
        return jnp.where(leading, upper, lower)

    tap_sum = halving_scatter(select(earlier[3], later[3]), "ctx")
    outputs = select(first_out, second_out)[None]
    grad_q = select(earlier[0], later[0])[None]
    grad_k = select(earlier[1], later[1])[None]
    grad_input = select(earlier[2], later[2])[None]
    return (outputs, grad_q, grad_k, grad_input, tap_sum[None])


def solution(mesh):
    return jax.shard_map(
        body,
        mesh=mesh,
        in_specs=(
            P("section", "ctx", "chan"),
            P("section", "ctx", "chan"),
            P("ctx", "chan"),
            P("ctx", "chan"),
            P("section", None, None, "chan"),
            P("section", None, "chan"),
            P("section", "chan"),
        ),
        out_specs=(
            P("section", "ctx", "chan"),
            P("section", "ctx", "chan"),
            P("section", "ctx", "chan"),
            P("section", "ctx", "chan"),
            P("section", "ctx", "chan"),
        ),
        check_vma=False,
    )
```

```python
import jax
import jax.numpy as jnp
from jax import lax
from jax.sharding import PartitionSpec as P


def shifted(value, axis, by):
    peers = lax.axis_size(axis)
    pairs = [(i, i + by) for i in range(peers) if 0 <= i + by < peers]
    return lax.ppermute(value, axis, pairs)


def halving_scatter(part, axis):
    peers = lax.axis_size(axis)
    steps = peers.bit_length() - 1
    if peers != 1 << steps or part.shape[0] % peers:
        return lax.psum_scatter(part, axis, scatter_dimension=0, tiled=True)
    me = lax.axis_index(axis)
    rows = part.shape[0] // peers
    held = part.reshape((2,) * steps + (rows,) + part.shape[1:])
    remaining = [steps - 1 - k for k in range(steps)]
    order = [0, 2, 1, 3, 4] if steps == 5 else list(range(steps))
    for bit in order:
        at = remaining.index(bit)
        mine = (me >> bit) & 1
        keep = lax.dynamic_index_in_dim(held, mine, axis=at, keepdims=False)
        give = lax.dynamic_index_in_dim(held, 1 - mine, axis=at, keepdims=False)
        got = lax.ppermute(give, axis, [(i, i ^ (1 << bit)) for i in range(peers)])
        held = keep + got
        remaining.pop(at)
    return held.reshape((rows,) + part.shape[1:])


def depthwise(source, kernel):
    result = lax.conv_general_dilated(
        source[None],
        kernel[:, None, :],
        (1,),
        "VALID",
        dimension_numbers=("NWC", "WIO", "NWC"),
        feature_group_count=source.shape[1],
        preferred_element_type=jnp.float32,
    )
    return result[0]


def fwd_short(rows, weights):
    wide = rows.astype(jnp.float32)
    return weights[0] * wide[2:] + weights[1] * wide[1:-1] + weights[2] * wide[:-2]


def bwd_short(rows, weights):
    wide = rows.astype(jnp.float32)
    return weights[0] * wide[:-2] + weights[1] * wide[1:-1] + weights[2] * wide[2:]


def from_prev(value):
    return shifted(value, "ctx", 1)


def from_next(value):
    return shifted(value, "ctx", -1)


def body(queries, keys, values, cotangent, short_filter, mix_filter, skip):
    first = lax.axis_index("section") == 0
    q, k = queries[0], keys[0]
    w_q, w_k, w_v = short_filter[0][0], short_filter[0][1], short_filter[0][2]
    taps = mix_filter[0]
    extent = taps.shape[0]
    back = taps[::-1]
    skip_row = skip[0]
    rows = q.shape[0]
    reach = extent + 1

    prev_a = from_prev(jnp.concatenate([q[-2:], k[-reach:], values[-reach:]], axis=0))
    next_a = from_next(jnp.concatenate([q[:reach], k[:2], values[:2], cotangent[:reach]], axis=0))
    q_ext = jnp.concatenate([prev_a[:2], q, next_a[:reach]], axis=0)
    k_ext = jnp.concatenate([prev_a[2 : 2 + reach], k, next_a[reach : reach + 2]], axis=0)
    v_ext = jnp.concatenate([prev_a[2 + reach :], values, next_a[reach + 2 : reach + 4]], axis=0)
    g_ext = jnp.concatenate([cotangent, next_a[reach + 4 :]], axis=0)

    q_short = fwd_short(q_ext, w_q)
    k_short = fwd_short(k_ext, w_k)
    v_first = fwd_short(v_ext, w_v)
    u_first = (k_short * v_first).astype(jnp.bfloat16)
    gz_last = (g_ext.astype(jnp.float32) * q_short).astype(jnp.bfloat16)

    sig_a = jnp.where(first, u_first, gz_last)
    conv_a = depthwise(sig_a, jnp.where(first, back, taps)) + skip_row * jnp.where(
        first, u_first[extent - 1 :], gz_last[: rows + 2]
    ).astype(jnp.float32)
    out_first = (q_short[:rows] * conv_a[:rows]).astype(jnp.bfloat16)
    gvs_last = (conv_a * k_short[extent - 1 :]).astype(jnp.bfloat16)
    gin_last = bwd_short(gvs_last, w_v).astype(jnp.bfloat16)

    handed = lax.ppermute(jnp.where(first, out_first, gin_last), "section", [(0, 1), (1, 0)])
    prev_b = from_prev(handed[-reach:])
    next_b = from_next(handed[:reach])
    y_ext = jnp.concatenate([prev_b, handed, next_b], axis=0)

    gz_first = (y_ext[reach:].astype(jnp.float32) * q_short).astype(jnp.bfloat16)
    v_last = fwd_short(y_ext[: reach + rows + 2], w_v)
    u_last = (k_short * v_last).astype(jnp.bfloat16)
    sig_b = jnp.where(first, gz_first, u_last)
    conv_b = depthwise(sig_b, jnp.where(first, taps, back)) + skip_row * jnp.where(
        first, gz_first[: rows + 2], u_last[extent - 1 :]
    ).astype(jnp.float32)

    z = jnp.where(first, conv_a, conv_b)
    gu = jnp.where(first, conv_b, conv_a)
    v_short = jnp.where(first, v_first, v_last)
    u = jnp.where(first, u_first, u_last)
    g = jnp.where(first, y_ext[reach : reach + rows + 2], g_ext[: rows + 2]).astype(jnp.float32)
    gz = jnp.where(first, gz_first, gz_last)

    output = (q_short[:rows] * z[:rows]).astype(jnp.bfloat16)
    gqs = (g * z).astype(jnp.bfloat16)
    gks = (gu * v_short[extent - 1 :]).astype(jnp.bfloat16)
    gvs = (gu * k_short[extent - 1 :]).astype(jnp.bfloat16)
    grad_q = bwd_short(gqs, w_q).astype(jnp.bfloat16)
    grad_k = bwd_short(gks, w_k).astype(jnp.bfloat16)
    grad_input = bwd_short(gvs, w_v).astype(jnp.bfloat16)
    taps_part = depthwise(u[: rows + extent - 1], gz[:rows])[::-1]
    tap_sum = halving_scatter(taps_part, "ctx")
    return (output[None], grad_q[None], grad_k[None], grad_input[None], tap_sum[None])


def solution(mesh):
    return jax.shard_map(
        body,
        mesh=mesh,
        in_specs=(
            P("section", "ctx", "chan"),
            P("section", "ctx", "chan"),
            P("ctx", "chan"),
            P("ctx", "chan"),
            P("section", None, None, "chan"),
            P("section", None, "chan"),
            P("section", "chan"),
        ),
        out_specs=(
            P("section", "ctx", "chan"),
            P("section", "ctx", "chan"),
            P("section", "ctx", "chan"),
            P("section", "ctx", "chan"),
            P("section", "ctx", "chan"),
        ),
        check_vma=False,
    )
```

```python
import jax
import jax.numpy as jnp
from jax import lax
from jax.sharding import PartitionSpec as P


def shifted(value, axis, by):
    peers = lax.axis_size(axis)
    pairs = [(i, i + by) for i in range(peers) if 0 <= i + by < peers]
    return lax.ppermute(value, axis, pairs)


def halving_scatter(part, axis):
    peers = lax.axis_size(axis)
    steps = peers.bit_length() - 1
    if peers != 1 << steps or part.shape[0] % peers:
        return lax.psum_scatter(part, axis, scatter_dimension=0, tiled=True)
    me = lax.axis_index(axis)
    rows = part.shape[0] // peers
    held = part.reshape((2,) * steps + (rows,) + part.shape[1:])
    remaining = [steps - 1 - k for k in range(steps)]
    order = [0, 2, 1, 3, 4] if steps == 5 else list(range(steps))
    for bit in order:
        at = remaining.index(bit)
        mine = (me >> bit) & 1
        keep = lax.dynamic_index_in_dim(held, mine, axis=at, keepdims=False)
        give = lax.dynamic_index_in_dim(held, 1 - mine, axis=at, keepdims=False)
        got = lax.ppermute(give, axis, [(i, i ^ (1 << bit)) for i in range(peers)])
        held = keep + got
        remaining.pop(at)
    return held.reshape((rows,) + part.shape[1:])


def depthwise(source, kernel):
    result = lax.conv_general_dilated(
        source[None],
        kernel[:, None, :],
        (1,),
        "VALID",
        dimension_numbers=("NWC", "WIO", "NWC"),
        feature_group_count=source.shape[1],
        preferred_element_type=jnp.float32,
    )
    return result[0]


def fwd_short(rows, weights):
    wide = rows.astype(jnp.float32)
    return weights[0] * wide[2:] + weights[1] * wide[1:-1] + weights[2] * wide[:-2]


def bwd_short(rows, weights):
    wide = rows.astype(jnp.float32)
    return weights[0] * wide[:-2] + weights[1] * wide[1:-1] + weights[2] * wide[2:]


def from_prev(value):
    return shifted(value, "ctx", 1)


def from_next(value):
    return shifted(value, "ctx", -1)


def body(queries, keys, values, cotangent, short_filter, mix_filter, skip):
    first = lax.axis_index("section") == 0
    q, k = queries[0], keys[0]
    w_q, w_k, w_v = short_filter[0][0], short_filter[0][1], short_filter[0][2]
    taps = mix_filter[0]
    extent = taps.shape[0]
    back = taps[::-1]
    skip_row = skip[0]
    rows = q.shape[0]
    reach = extent + 1

    prev_a = from_prev(jnp.concatenate([q[-2:], k[-reach:], values[-reach:]], axis=0))
    next_a = from_next(jnp.concatenate([q[:reach], k[:2], values[:2], cotangent[:reach]], axis=0))
    q_ext = jnp.concatenate([prev_a[:2], q, next_a[:reach]], axis=0)
    k_ext = jnp.concatenate([prev_a[2 : 2 + reach], k, next_a[reach : reach + 2]], axis=0)
    v_ext = jnp.concatenate([prev_a[2 + reach :], values, next_a[reach + 2 : reach + 4]], axis=0)
    g_ext = jnp.concatenate([cotangent, next_a[reach + 4 :]], axis=0)

    q_short = fwd_short(q_ext, w_q)
    k_short = fwd_short(k_ext, w_k)
    v_first = fwd_short(v_ext, w_v)
    u_first = (k_short * v_first).astype(jnp.bfloat16)
    gz_last = (g_ext.astype(jnp.float32) * q_short).astype(jnp.bfloat16)

    sig_a = jnp.where(first, u_first, gz_last)
    conv_a = depthwise(sig_a, jnp.where(first, back, taps)) + skip_row * jnp.where(
        first, u_first[extent - 1 :], gz_last[: rows + 2]
    ).astype(jnp.float32)
    out_first = (q_short[:rows] * conv_a[:rows]).astype(jnp.bfloat16)
    gvs_last = (conv_a * k_short[extent - 1 :]).astype(jnp.bfloat16)
    gin_last = bwd_short(gvs_last, w_v).astype(jnp.bfloat16)

    handed = lax.ppermute(jnp.where(first, out_first, gin_last), "section", [(0, 1), (1, 0)])
    prev_b = from_prev(handed[-reach:])
    next_b = from_next(handed[:reach])
    y_ext = jnp.concatenate([prev_b, handed, next_b], axis=0)

    gz_first = (y_ext[reach:].astype(jnp.float32) * q_short).astype(jnp.bfloat16)
    v_last = fwd_short(y_ext[: reach + rows + 2], w_v)
    u_last = (k_short * v_last).astype(jnp.bfloat16)
    sig_b = jnp.where(first, gz_first, u_last)
    conv_b = depthwise(sig_b, jnp.where(first, taps, back)) + skip_row * jnp.where(
        first, gz_first[: rows + 2], u_last[extent - 1 :]
    ).astype(jnp.float32)

    z = jnp.where(first, conv_a, conv_b)
    gu = jnp.where(first, conv_b, conv_a)
    v_short = jnp.where(first, v_first, v_last)
    u = jnp.where(first, u_first, u_last)
    g = jnp.where(first, y_ext[reach : reach + rows + 2], g_ext[: rows + 2]).astype(jnp.float32)
    gz = jnp.where(first, gz_first, gz_last)

    output = (q_short[:rows] * z[:rows]).astype(jnp.bfloat16)
    gqs = (g * z).astype(jnp.bfloat16)
    gks = (gu * v_short[extent - 1 :]).astype(jnp.bfloat16)
    gvs = (gu * k_short[extent - 1 :]).astype(jnp.bfloat16)
    grad_q = bwd_short(gqs, w_q).astype(jnp.bfloat16)
    grad_k = bwd_short(gks, w_k).astype(jnp.bfloat16)
    grad_input = bwd_short(gvs, w_v).astype(jnp.bfloat16)
    taps_part = depthwise(u[: rows + extent - 1], gz[:rows])[::-1]
    tap_sum = halving_scatter(taps_part, "ctx")
    return (output[None], grad_q[None], grad_k[None], grad_input[None], tap_sum[None])


def chunked(*args, pieces=2):
    width = args[0].shape[-1]
    if width % (pieces * 128):
        return body(*args)
    step = width // pieces
    parts = []
    for i in range(pieces):
        parts.append(body(*(a[..., i * step : (i + 1) * step] for a in args)))
    return tuple(jnp.concatenate(group, axis=-1) for group in zip(*parts))


def solution(mesh):
    return jax.shard_map(
        chunked,
        mesh=mesh,
        in_specs=(
            P("section", "ctx", "chan"),
            P("section", "ctx", "chan"),
            P("ctx", "chan"),
            P("ctx", "chan"),
            P("section", None, None, "chan"),
            P("section", None, "chan"),
            P("section", "chan"),
        ),
        out_specs=(
            P("section", "ctx", "chan"),
            P("section", "ctx", "chan"),
            P("section", "ctx", "chan"),
            P("section", "ctx", "chan"),
            P("section", "ctx", "chan"),
        ),
        check_vma=False,
    )
```

```python
import jax
import jax.numpy as jnp
from jax import lax
from jax.sharding import PartitionSpec as P


def shifted(value, axis, by):
    peers = lax.axis_size(axis)
    pairs = [(i, i + by) for i in range(peers) if 0 <= i + by < peers]
    return lax.ppermute(value, axis, pairs)


def halving_scatter(part, axis):
    peers = lax.axis_size(axis)
    steps = peers.bit_length() - 1
    if peers != 1 << steps or part.shape[0] % peers:
        return lax.psum_scatter(part, axis, scatter_dimension=0, tiled=True)
    me = lax.axis_index(axis)
    rows = part.shape[0] // peers
    held = part.reshape((2,) * steps + (rows,) + part.shape[1:])
    remaining = [steps - 1 - k for k in range(steps)]
    order = [0, 2, 1, 3, 4] if steps == 5 else list(range(steps))
    for bit in order:
        at = remaining.index(bit)
        mine = (me >> bit) & 1
        keep = lax.dynamic_index_in_dim(held, mine, axis=at, keepdims=False)
        give = lax.dynamic_index_in_dim(held, 1 - mine, axis=at, keepdims=False)
        got = lax.ppermute(give, axis, [(i, i ^ (1 << bit)) for i in range(peers)])
        held = keep + got
        remaining.pop(at)
    return held.reshape((rows,) + part.shape[1:])


def exchange_scatter(part, axis):
    peers = lax.axis_size(axis)
    if part.shape[0] % peers:
        return lax.psum_scatter(part, axis, scatter_dimension=0, tiled=True)
    rows = part.shape[0] // peers
    pieces = part.reshape((peers, rows) + part.shape[1:])
    got = lax.all_to_all(pieces, axis, 0, 0)
    return jnp.sum(got, axis=0)


def depthwise(source, kernel):
    result = lax.conv_general_dilated(
        source[None],
        kernel[:, None, :],
        (1,),
        "VALID",
        dimension_numbers=("NWC", "WIO", "NWC"),
        feature_group_count=source.shape[1],
        preferred_element_type=jnp.float32,
    )
    return result[0]


def fwd_short(rows, weights):
    wide = rows.astype(jnp.float32)
    return weights[0] * wide[2:] + weights[1] * wide[1:-1] + weights[2] * wide[:-2]


def bwd_short(rows, weights):
    wide = rows.astype(jnp.float32)
    return weights[0] * wide[:-2] + weights[1] * wide[1:-1] + weights[2] * wide[2:]


def from_prev(value):
    return shifted(value, "ctx", 1)


def from_next(value):
    return shifted(value, "ctx", -1)


def body(queries, keys, values, cotangent, short_filter, mix_filter, skip):
    first = lax.axis_index("section") == 0
    q, k = queries[0], keys[0]
    w_q, w_k, w_v = short_filter[0][0], short_filter[0][1], short_filter[0][2]
    taps = mix_filter[0]
    extent = taps.shape[0]
    back = taps[::-1]
    skip_row = skip[0]
    rows = q.shape[0]
    reach = extent + 1

    prev_a = from_prev(jnp.concatenate([q[-2:], k[-reach:], values[-reach:]], axis=0))
    next_a = from_next(jnp.concatenate([q[:reach], k[:2], values[:2], cotangent[:reach]], axis=0))
    q_ext = jnp.concatenate([prev_a[:2], q, next_a[:reach]], axis=0)
    k_ext = jnp.concatenate([prev_a[2 : 2 + reach], k, next_a[reach : reach + 2]], axis=0)
    v_ext = jnp.concatenate([prev_a[2 + reach :], values, next_a[reach + 2 : reach + 4]], axis=0)
    g_ext = jnp.concatenate([cotangent, next_a[reach + 4 :]], axis=0)

    q_short = fwd_short(q_ext, w_q)
    k_short = fwd_short(k_ext, w_k)
    v_first = fwd_short(v_ext, w_v)
    u_first = (k_short * v_first).astype(jnp.bfloat16)
    gz_last = (g_ext.astype(jnp.float32) * q_short).astype(jnp.bfloat16)

    sig_a = jnp.where(first, u_first, gz_last)
    conv_a = depthwise(sig_a, jnp.where(first, back, taps)) + skip_row * jnp.where(
        first, u_first[extent - 1 :], gz_last[: rows + 2]
    ).astype(jnp.float32)
    out_first = (q_short[:rows] * conv_a[:rows]).astype(jnp.bfloat16)
    gvs_last = (conv_a * k_short[extent - 1 :]).astype(jnp.bfloat16)
    gin_last = bwd_short(gvs_last, w_v).astype(jnp.bfloat16)

    handed = lax.ppermute(jnp.where(first, out_first, gin_last), "section", [(0, 1), (1, 0)])
    prev_b = from_prev(handed[-reach:])
    next_b = from_next(handed[:reach])
    y_ext = jnp.concatenate([prev_b, handed, next_b], axis=0)

    gz_first = (y_ext[reach:].astype(jnp.float32) * q_short).astype(jnp.bfloat16)
    v_last = fwd_short(y_ext[: reach + rows + 2], w_v)
    u_last = (k_short * v_last).astype(jnp.bfloat16)
    sig_b = jnp.where(first, gz_first, u_last)
    conv_b = depthwise(sig_b, jnp.where(first, taps, back)) + skip_row * jnp.where(
        first, gz_first[: rows + 2], u_last[extent - 1 :]
    ).astype(jnp.float32)

    z = jnp.where(first, conv_a, conv_b)
    gu = jnp.where(first, conv_b, conv_a)
    v_short = jnp.where(first, v_first, v_last)
    u = jnp.where(first, u_first, u_last)
    g = jnp.where(first, y_ext[reach : reach + rows + 2], g_ext[: rows + 2]).astype(jnp.float32)
    gz = jnp.where(first, gz_first, gz_last)

    output = (q_short[:rows] * z[:rows]).astype(jnp.bfloat16)
    gqs = (g * z).astype(jnp.bfloat16)
    gks = (gu * v_short[extent - 1 :]).astype(jnp.bfloat16)
    gvs = (gu * k_short[extent - 1 :]).astype(jnp.bfloat16)
    grad_q = bwd_short(gqs, w_q).astype(jnp.bfloat16)
    grad_k = bwd_short(gks, w_k).astype(jnp.bfloat16)
    grad_input = bwd_short(gvs, w_v).astype(jnp.bfloat16)
    taps_part = depthwise(u[: rows + extent - 1], gz[:rows])[::-1]
    tap_sum = exchange_scatter(taps_part, "ctx")
    return (output[None], grad_q[None], grad_k[None], grad_input[None], tap_sum[None])


def solution(mesh):
    return jax.shard_map(
        body,
        mesh=mesh,
        in_specs=(
            P("section", "ctx", "chan"),
            P("section", "ctx", "chan"),
            P("ctx", "chan"),
            P("ctx", "chan"),
            P("section", None, None, "chan"),
            P("section", None, "chan"),
            P("section", "chan"),
        ),
        out_specs=(
            P("section", "ctx", "chan"),
            P("section", "ctx", "chan"),
            P("section", "ctx", "chan"),
            P("section", "ctx", "chan"),
            P("section", "ctx", "chan"),
        ),
        check_vma=False,
    )
```

```python
import jax
import jax.numpy as jnp
from jax import lax
from jax.sharding import PartitionSpec as P


def shifted(value, axis, by):
    peers = lax.axis_size(axis)
    pairs = [(i, i + by) for i in range(peers) if 0 <= i + by < peers]
    return lax.ppermute(value, axis, pairs)


def halving_scatter(part, axis):
    peers = lax.axis_size(axis)
    steps = peers.bit_length() - 1
    if peers != 1 << steps or part.shape[0] % peers:
        return lax.psum_scatter(part, axis, scatter_dimension=0, tiled=True)
    me = lax.axis_index(axis)
    rows = part.shape[0] // peers
    held = part.reshape((2,) * steps + (rows,) + part.shape[1:])
    remaining = [steps - 1 - k for k in range(steps)]
    order = [0, 2, 1, 3, 4] if steps == 5 else list(range(steps))
    for bit in order:
        at = remaining.index(bit)
        mine = (me >> bit) & 1
        keep = lax.dynamic_index_in_dim(held, mine, axis=at, keepdims=False)
        give = lax.dynamic_index_in_dim(held, 1 - mine, axis=at, keepdims=False)
        got = lax.ppermute(give, axis, [(i, i ^ (1 << bit)) for i in range(peers)])
        held = keep + got
        remaining.pop(at)
    return held.reshape((rows,) + part.shape[1:])


def exchange_scatter(part, axis):
    peers = lax.axis_size(axis)
    if part.shape[0] % peers:
        return lax.psum_scatter(part[::-1], axis, scatter_dimension=0, tiled=True)
    rows = part.shape[0] // peers
    pieces = part.reshape((peers, rows) + part.shape[1:])[::-1]
    got = lax.all_to_all(pieces, axis, 0, 0)
    return jnp.sum(got, axis=0)[::-1]


def depthwise(source, kernel):
    result = lax.conv_general_dilated(
        source[None],
        kernel[:, None, :],
        (1,),
        "VALID",
        dimension_numbers=("NWC", "WIO", "NWC"),
        feature_group_count=source.shape[1],
        preferred_element_type=jnp.float32,
    )
    return result[0]


def fwd_short(rows, weights):
    wide = rows.astype(jnp.float32)
    return weights[0] * wide[2:] + weights[1] * wide[1:-1] + weights[2] * wide[:-2]


def bwd_short(rows, weights):
    wide = rows.astype(jnp.float32)
    return weights[0] * wide[:-2] + weights[1] * wide[1:-1] + weights[2] * wide[2:]


def from_prev(value):
    return shifted(value, "ctx", 1)


def from_next(value):
    return shifted(value, "ctx", -1)


def body(queries, keys, values, cotangent, short_filter, mix_filter, skip):
    first = lax.axis_index("section") == 0
    q, k = queries[0], keys[0]
    w_q, w_k, w_v = short_filter[0][0], short_filter[0][1], short_filter[0][2]
    taps = mix_filter[0]
    extent = taps.shape[0]
    back = taps[::-1]
    skip_row = skip[0]
    rows = q.shape[0]
    reach = extent + 1

    prev_a = from_prev(jnp.concatenate([q[-2:], k[-reach:], values[-reach:]], axis=0))
    next_a = from_next(jnp.concatenate([q[:reach], k[:2], values[:2], cotangent[:reach]], axis=0))
    q_ext = jnp.concatenate([prev_a[:2], q, next_a[:reach]], axis=0)
    k_ext = jnp.concatenate([prev_a[2 : 2 + reach], k, next_a[reach : reach + 2]], axis=0)
    v_ext = jnp.concatenate([prev_a[2 + reach :], values, next_a[reach + 2 : reach + 4]], axis=0)
    g_ext = jnp.concatenate([cotangent, next_a[reach + 4 :]], axis=0)

    q_short = fwd_short(q_ext, w_q)
    k_short = fwd_short(k_ext, w_k)
    v_first = fwd_short(v_ext, w_v)
    u_first = (k_short * v_first).astype(jnp.bfloat16)
    gz_last = (g_ext.astype(jnp.float32) * q_short).astype(jnp.bfloat16)

    sig_a = jnp.where(first, u_first, gz_last)
    conv_a = depthwise(sig_a, jnp.where(first, back, taps)) + skip_row * jnp.where(
        first, u_first[extent - 1 :], gz_last[: rows + 2]
    ).astype(jnp.float32)
    out_first = (q_short[:rows] * conv_a[:rows]).astype(jnp.bfloat16)
    gvs_last = (conv_a * k_short[extent - 1 :]).astype(jnp.bfloat16)
    gin_last = bwd_short(gvs_last, w_v).astype(jnp.bfloat16)

    handed = lax.ppermute(jnp.where(first, out_first, gin_last), "section", [(0, 1), (1, 0)])
    prev_b = from_prev(handed[-reach:])
    next_b = from_next(handed[:reach])
    y_ext = jnp.concatenate([prev_b, handed, next_b], axis=0)

    gz_first = (y_ext[reach:].astype(jnp.float32) * q_short).astype(jnp.bfloat16)
    v_last = fwd_short(y_ext[: reach + rows + 2], w_v)
    u_last = (k_short * v_last).astype(jnp.bfloat16)
    sig_b = jnp.where(first, gz_first, u_last)
    conv_b = depthwise(sig_b, jnp.where(first, taps, back)) + skip_row * jnp.where(
        first, gz_first[: rows + 2], u_last[extent - 1 :]
    ).astype(jnp.float32)

    z = jnp.where(first, conv_a, conv_b)
    gu = jnp.where(first, conv_b, conv_a)
    v_short = jnp.where(first, v_first, v_last)
    u = jnp.where(first, u_first, u_last)
    g = jnp.where(first, y_ext[reach : reach + rows + 2], g_ext[: rows + 2]).astype(jnp.float32)
    gz = jnp.where(first, gz_first, gz_last)

    output = (q_short[:rows] * z[:rows]).astype(jnp.bfloat16)
    gqs = (g * z).astype(jnp.bfloat16)
    gks = (gu * v_short[extent - 1 :]).astype(jnp.bfloat16)
    gvs = (gu * k_short[extent - 1 :]).astype(jnp.bfloat16)
    grad_q = bwd_short(gqs, w_q).astype(jnp.bfloat16)
    grad_k = bwd_short(gks, w_k).astype(jnp.bfloat16)
    grad_input = bwd_short(gvs, w_v).astype(jnp.bfloat16)
    lags = depthwise(u[: rows + extent - 1], gz[:rows])
    lags, output, grad_q, grad_k, grad_input = lax.optimization_barrier(
        (lags, output, grad_q, grad_k, grad_input)
    )
    tap_sum = exchange_scatter(lags, "ctx")
    return (output[None], grad_q[None], grad_k[None], grad_input[None], tap_sum[None])


def solution(mesh):
    return jax.shard_map(
        body,
        mesh=mesh,
        in_specs=(
            P("section", "ctx", "chan"),
            P("section", "ctx", "chan"),
            P("ctx", "chan"),
            P("ctx", "chan"),
            P("section", None, None, "chan"),
            P("section", None, "chan"),
            P("section", "chan"),
        ),
        out_specs=(
            P("section", "ctx", "chan"),
            P("section", "ctx", "chan"),
            P("section", "ctx", "chan"),
            P("section", "ctx", "chan"),
            P("section", "ctx", "chan"),
        ),
        check_vma=False,
    )
```

```python
import jax
import jax.numpy as jnp
from jax import lax
from jax.sharding import PartitionSpec as P


def shifted(value, axis, by):
    peers = lax.axis_size(axis)
    pairs = [(i, i + by) for i in range(peers) if 0 <= i + by < peers]
    return lax.ppermute(value, axis, pairs)


def halving_scatter(part, axis):
    peers = lax.axis_size(axis)
    steps = peers.bit_length() - 1
    if peers != 1 << steps or part.shape[0] % peers:
        return lax.psum_scatter(part, axis, scatter_dimension=0, tiled=True)
    me = lax.axis_index(axis)
    rows = part.shape[0] // peers
    held = part.reshape((2,) * steps + (rows,) + part.shape[1:])
    remaining = [steps - 1 - k for k in range(steps)]
    order = [0, 2, 1, 3, 4] if steps == 5 else list(range(steps))
    for bit in order:
        at = remaining.index(bit)
        mine = (me >> bit) & 1
        keep = lax.dynamic_index_in_dim(held, mine, axis=at, keepdims=False)
        give = lax.dynamic_index_in_dim(held, 1 - mine, axis=at, keepdims=False)
        got = lax.ppermute(give, axis, [(i, i ^ (1 << bit)) for i in range(peers)])
        held = keep + got
        remaining.pop(at)
    return held.reshape((rows,) + part.shape[1:])


def exchange_scatter(part, axis):
    peers = lax.axis_size(axis)
    if part.shape[0] % peers:
        return lax.psum_scatter(part[::-1], axis, scatter_dimension=0, tiled=True)
    rows = part.shape[0] // peers
    pieces = part.reshape((peers, rows) + part.shape[1:])[::-1]
    got = lax.all_to_all(pieces, axis, 0, 0)
    return jnp.sum(got, axis=0)[::-1]


def depthwise(source, kernel):
    result = lax.conv_general_dilated(
        source[None],
        kernel[:, None, :],
        (1,),
        "VALID",
        dimension_numbers=("NWC", "WIO", "NWC"),
        feature_group_count=source.shape[1],
        preferred_element_type=jnp.float32,
    )
    return result[0]


def fwd_short(rows, weights):
    wide = rows.astype(jnp.float32)
    return weights[0] * wide[2:] + weights[1] * wide[1:-1] + weights[2] * wide[:-2]


def bwd_short(rows, weights):
    wide = rows.astype(jnp.float32)
    return weights[0] * wide[:-2] + weights[1] * wide[1:-1] + weights[2] * wide[2:]


def from_prev(value):
    return shifted(value, "ctx", 1)


def from_next(value):
    return shifted(value, "ctx", -1)


def body(queries, keys, values, cotangent, short_filter, mix_filter, skip):
    first = lax.axis_index("section") == 0
    q, k = queries[0], keys[0]
    w_q, w_k, w_v = short_filter[0][0], short_filter[0][1], short_filter[0][2]
    taps = mix_filter[0]
    extent = taps.shape[0]
    back = taps[::-1]
    skip_row = skip[0]
    rows = q.shape[0]
    reach = extent + 1

    prev_a = from_prev(jnp.concatenate([q[-2:], k[-reach:], values[-reach:]], axis=0))
    next_a = from_next(jnp.concatenate([q[:reach], k[:2], values[:2], cotangent[:reach]], axis=0))
    q_ext = jnp.concatenate([prev_a[:2], q, next_a[:reach]], axis=0)
    k_ext = jnp.concatenate([prev_a[2 : 2 + reach], k, next_a[reach : reach + 2]], axis=0)
    v_ext = jnp.concatenate([prev_a[2 + reach :], values, next_a[reach + 2 : reach + 4]], axis=0)
    g_ext = jnp.concatenate([cotangent, next_a[reach + 4 :]], axis=0)

    q_short = fwd_short(q_ext, w_q)
    k_short = fwd_short(k_ext, w_k)
    v_first = fwd_short(v_ext, w_v)
    u_first = (k_short * v_first).astype(jnp.bfloat16)
    gz_last = (g_ext.astype(jnp.float32) * q_short).astype(jnp.bfloat16)

    sig_a = jnp.where(first, u_first, gz_last)
    conv_a = depthwise(sig_a, jnp.where(first, back, taps)) + skip_row * jnp.where(
        first, u_first[extent - 1 :], gz_last[: rows + 2]
    ).astype(jnp.float32)
    out_first = (q_short[:rows] * conv_a[:rows]).astype(jnp.bfloat16)
    gvs_last = (conv_a * k_short[extent - 1 :]).astype(jnp.bfloat16)
    gin_last = bwd_short(gvs_last, w_v).astype(jnp.bfloat16)

    handed = lax.ppermute(jnp.where(first, out_first, gin_last), "section", [(0, 1), (1, 0)])
    prev_b = from_prev(handed[-reach:])
    next_b = from_next(handed[:reach])
    y_ext = jnp.concatenate([prev_b, handed, next_b], axis=0)

    gz_first = (y_ext[reach:].astype(jnp.float32) * q_short).astype(jnp.bfloat16)
    v_last = fwd_short(y_ext[: reach + rows + 2], w_v)
    u_last = (k_short * v_last).astype(jnp.bfloat16)
    sig_b = jnp.where(first, gz_first, u_last)
    conv_b = depthwise(sig_b, jnp.where(first, taps, back)) + skip_row * jnp.where(
        first, gz_first[: rows + 2], u_last[extent - 1 :]
    ).astype(jnp.float32)

    z = jnp.where(first, conv_a, conv_b)
    gu = jnp.where(first, conv_b, conv_a)
    v_short = jnp.where(first, v_first, v_last)
    u = jnp.where(first, u_first, u_last)
    g = jnp.where(first, y_ext[reach : reach + rows + 2], g_ext[: rows + 2]).astype(jnp.float32)
    gz = jnp.where(first, gz_first, gz_last)

    output = (q_short[:rows] * z[:rows]).astype(jnp.bfloat16)
    gqs = (g * z).astype(jnp.bfloat16)
    gks = (gu * v_short[extent - 1 :]).astype(jnp.bfloat16)
    gvs = (gu * k_short[extent - 1 :]).astype(jnp.bfloat16)
    grad_q = bwd_short(gqs, w_q).astype(jnp.bfloat16)
    grad_k = bwd_short(gks, w_k).astype(jnp.bfloat16)
    grad_input = bwd_short(gvs, w_v).astype(jnp.bfloat16)
    lags = depthwise(u[: rows + extent - 1], gz[:rows])
    tap_sum = exchange_scatter(lags, "ctx")
    return (output[None], grad_q[None], grad_k[None], grad_input[None], tap_sum[None])


def solution(mesh):
    return jax.shard_map(
        body,
        mesh=mesh,
        in_specs=(
            P("section", "ctx", "chan"),
            P("section", "ctx", "chan"),
            P("ctx", "chan"),
            P("ctx", "chan"),
            P("section", None, None, "chan"),
            P("section", None, "chan"),
            P("section", "chan"),
        ),
        out_specs=(
            P("section", "ctx", "chan"),
            P("section", "ctx", "chan"),
            P("section", "ctx", "chan"),
            P("section", "ctx", "chan"),
            P("section", "ctx", "chan"),
        ),
        check_vma=False,
    )
```

```python
import jax
import jax.numpy as jnp
from jax import lax
from jax.sharding import PartitionSpec as P


def shifted(value, axis, by):
    peers = lax.axis_size(axis)
    pairs = [(i, i + by) for i in range(peers) if 0 <= i + by < peers]
    return lax.ppermute(value, axis, pairs)


def halving_scatter(part, axis):
    peers = lax.axis_size(axis)
    steps = peers.bit_length() - 1
    if peers != 1 << steps or part.shape[0] % peers:
        return lax.psum_scatter(part, axis, scatter_dimension=0, tiled=True)
    me = lax.axis_index(axis)
    rows = part.shape[0] // peers
    held = part.reshape((2,) * steps + (rows,) + part.shape[1:])
    remaining = [steps - 1 - k for k in range(steps)]
    order = [0, 2, 1, 3, 4] if steps == 5 else list(range(steps))
    for bit in order:
        at = remaining.index(bit)
        mine = (me >> bit) & 1
        keep = lax.dynamic_index_in_dim(held, mine, axis=at, keepdims=False)
        give = lax.dynamic_index_in_dim(held, 1 - mine, axis=at, keepdims=False)
        got = lax.ppermute(give, axis, [(i, i ^ (1 << bit)) for i in range(peers)])
        held = keep + got
        remaining.pop(at)
    return held.reshape((rows,) + part.shape[1:])


def exchange_scatter(part, axis):
    peers = lax.axis_size(axis)
    if part.shape[0] % peers:
        return lax.psum_scatter(part, axis, scatter_dimension=0, tiled=True)
    rows = part.shape[0] // peers
    pieces = part.reshape((peers, rows) + part.shape[1:])
    got = lax.all_to_all(pieces, axis, 0, 0)
    return jnp.sum(got, axis=0)


def depthwise(source, kernel):
    result = lax.conv_general_dilated(
        source[None],
        kernel[:, None, :],
        (1,),
        "VALID",
        dimension_numbers=("NWC", "WIO", "NWC"),
        feature_group_count=source.shape[1],
        preferred_element_type=jnp.float32,
    )
    return result[0]


def fwd_short(rows, weights):
    wide = rows.astype(jnp.float32)
    return weights[0] * wide[2:] + weights[1] * wide[1:-1] + weights[2] * wide[:-2]


def bwd_short(rows, weights):
    wide = rows.astype(jnp.float32)
    return weights[0] * wide[:-2] + weights[1] * wide[1:-1] + weights[2] * wide[2:]


def from_prev(value):
    return shifted(value, "ctx", 1)


def from_next(value):
    return shifted(value, "ctx", -1)


def body(queries, keys, values, cotangent, short_filter, mix_filter, skip):
    first = lax.axis_index("section") == 0
    q, k = queries[0], keys[0]
    w_q, w_k, w_v = short_filter[0][0], short_filter[0][1], short_filter[0][2]
    taps = mix_filter[0]
    extent = taps.shape[0]
    back = taps[::-1]
    skip_row = skip[0]
    rows = q.shape[0]
    reach = extent + 1

    prev_a = from_prev(jnp.concatenate([q[-2:], k[-reach:], values[-reach:]], axis=0))
    next_a = from_next(jnp.concatenate([q[:reach], k[:2], values[:2], cotangent[:reach]], axis=0))
    q_ext = jnp.concatenate([prev_a[:2], q, next_a[:reach]], axis=0)
    k_ext = jnp.concatenate([prev_a[2 : 2 + reach], k, next_a[reach : reach + 2]], axis=0)
    v_ext = jnp.concatenate([prev_a[2 + reach :], values, next_a[reach + 2 : reach + 4]], axis=0)
    g_ext = jnp.concatenate([cotangent, next_a[reach + 4 :]], axis=0)

    q_short = fwd_short(q_ext, w_q)
    k_short = fwd_short(k_ext, w_k)
    v_first = fwd_short(v_ext, w_v)
    u_first = (k_short * v_first).astype(jnp.bfloat16)
    gz_last = (g_ext.astype(jnp.float32) * q_short).astype(jnp.bfloat16)

    sig_a = jnp.where(first, u_first, gz_last)
    conv_a = depthwise(sig_a, jnp.where(first, back, taps)) + skip_row * jnp.where(
        first, u_first[extent - 1 :], gz_last[: rows + 2]
    ).astype(jnp.float32)
    out_first = (q_short[:rows] * conv_a[:rows]).astype(jnp.bfloat16)
    gvs_last = (conv_a * k_short[extent - 1 :]).astype(jnp.bfloat16)
    gin_last = bwd_short(gvs_last, w_v).astype(jnp.bfloat16)

    handed = lax.ppermute(jnp.where(first, out_first, gin_last), "section", [(0, 1), (1, 0)])
    sections = lax.axis_size("section")
    peers = lax.axis_size("ctx")
    both = ("section", "ctx")
    rim = lax.ppermute(
        jnp.where(first, out_first[-reach:], gin_last[:reach]),
        both,
        [(i, peers + i + 1) for i in range(peers - 1)] + [(peers + i, i - 1) for i in range(1, peers)],
    ) if sections == 2 else None
    if rim is None:
        prev_b = from_prev(handed[-reach:])
        next_b = from_next(handed[:reach])
    else:
        ahead = lax.ppermute(out_first[:2], both, [(i + 1, peers + i) for i in range(peers - 1)])
        prev_b = rim
        next_b = jnp.concatenate([jnp.where(first, rim[:2], ahead), rim[2:]], axis=0)
    y_ext = jnp.concatenate([prev_b, handed, next_b], axis=0)

    gz_first = (y_ext[reach:].astype(jnp.float32) * q_short).astype(jnp.bfloat16)
    v_last = fwd_short(y_ext[: reach + rows + 2], w_v)
    u_last = (k_short * v_last).astype(jnp.bfloat16)
    sig_b = jnp.where(first, gz_first, u_last)
    conv_b = depthwise(sig_b, jnp.where(first, taps, back)) + skip_row * jnp.where(
        first, gz_first[: rows + 2], u_last[extent - 1 :]
    ).astype(jnp.float32)

    z = jnp.where(first, conv_a, conv_b)
    gu = jnp.where(first, conv_b, conv_a)
    v_short = jnp.where(first, v_first, v_last)
    u = jnp.where(first, u_first, u_last)
    g = jnp.where(first, y_ext[reach : reach + rows + 2], g_ext[: rows + 2]).astype(jnp.float32)
    gz = jnp.where(first, gz_first, gz_last)

    output = (q_short[:rows] * z[:rows]).astype(jnp.bfloat16)
    gqs = (g * z).astype(jnp.bfloat16)
    gks = (gu * v_short[extent - 1 :]).astype(jnp.bfloat16)
    gvs = (gu * k_short[extent - 1 :]).astype(jnp.bfloat16)
    grad_q = bwd_short(gqs, w_q).astype(jnp.bfloat16)
    grad_k = bwd_short(gks, w_k).astype(jnp.bfloat16)
    grad_input = bwd_short(gvs, w_v).astype(jnp.bfloat16)
    taps_part = depthwise(u[: rows + extent - 1], gz[:rows])[::-1]
    tap_sum = exchange_scatter(taps_part, "ctx")
    return (output[None], grad_q[None], grad_k[None], grad_input[None], tap_sum[None])


def solution(mesh):
    return jax.shard_map(
        body,
        mesh=mesh,
        in_specs=(
            P("section", "ctx", "chan"),
            P("section", "ctx", "chan"),
            P("ctx", "chan"),
            P("ctx", "chan"),
            P("section", None, None, "chan"),
            P("section", None, "chan"),
            P("section", "chan"),
        ),
        out_specs=(
            P("section", "ctx", "chan"),
            P("section", "ctx", "chan"),
            P("section", "ctx", "chan"),
            P("section", "ctx", "chan"),
            P("section", "ctx", "chan"),
        ),
        check_vma=False,
    )
```

```python
import jax
import jax.numpy as jnp
from jax import lax
from jax.sharding import PartitionSpec as P


def shifted(value, axis, by):
    peers = lax.axis_size(axis)
    pairs = [(i, i + by) for i in range(peers) if 0 <= i + by < peers]
    return lax.ppermute(value, axis, pairs)


def halving_scatter(part, axis):
    peers = lax.axis_size(axis)
    steps = peers.bit_length() - 1
    if peers != 1 << steps or part.shape[0] % peers:
        return lax.psum_scatter(part, axis, scatter_dimension=0, tiled=True)
    me = lax.axis_index(axis)
    rows = part.shape[0] // peers
    held = part.reshape((2,) * steps + (rows,) + part.shape[1:])
    remaining = [steps - 1 - k for k in range(steps)]
    order = [0, 2, 1, 3, 4] if steps == 5 else list(range(steps))
    for bit in order:
        at = remaining.index(bit)
        mine = (me >> bit) & 1
        keep = lax.dynamic_index_in_dim(held, mine, axis=at, keepdims=False)
        give = lax.dynamic_index_in_dim(held, 1 - mine, axis=at, keepdims=False)
        got = lax.ppermute(give, axis, [(i, i ^ (1 << bit)) for i in range(peers)])
        held = keep + got
        remaining.pop(at)
    return held.reshape((rows,) + part.shape[1:])


def exchange_scatter(part, axis):
    peers = lax.axis_size(axis)
    if part.shape[0] % peers:
        return lax.psum_scatter(part, axis, scatter_dimension=0, tiled=True)
    rows = part.shape[0] // peers
    pieces = part.reshape((peers, rows) + part.shape[1:])
    got = lax.all_to_all(pieces.astype(jnp.bfloat16), axis, 0, 0)
    return jnp.sum(got.astype(jnp.float32), axis=0)


def depthwise(source, kernel):
    result = lax.conv_general_dilated(
        source[None],
        kernel[:, None, :],
        (1,),
        "VALID",
        dimension_numbers=("NWC", "WIO", "NWC"),
        feature_group_count=source.shape[1],
        preferred_element_type=jnp.float32,
    )
    return result[0]


def fwd_short(rows, weights):
    wide = rows.astype(jnp.float32)
    return weights[0] * wide[2:] + weights[1] * wide[1:-1] + weights[2] * wide[:-2]


def bwd_short(rows, weights):
    wide = rows.astype(jnp.float32)
    return weights[0] * wide[:-2] + weights[1] * wide[1:-1] + weights[2] * wide[2:]


def from_prev(value):
    return shifted(value, "ctx", 1)


def from_next(value):
    return shifted(value, "ctx", -1)


def body(queries, keys, values, cotangent, short_filter, mix_filter, skip):
    first = lax.axis_index("section") == 0
    q, k = queries[0], keys[0]
    w_q, w_k, w_v = short_filter[0][0], short_filter[0][1], short_filter[0][2]
    taps = mix_filter[0]
    extent = taps.shape[0]
    back = taps[::-1]
    skip_row = skip[0]
    rows = q.shape[0]
    reach = extent + 1

    prev_a = from_prev(jnp.concatenate([q[-2:], k[-reach:], values[-reach:]], axis=0))
    next_a = from_next(jnp.concatenate([q[:reach], k[:2], values[:2], cotangent[:reach]], axis=0))
    q_ext = jnp.concatenate([prev_a[:2], q, next_a[:reach]], axis=0)
    k_ext = jnp.concatenate([prev_a[2 : 2 + reach], k, next_a[reach : reach + 2]], axis=0)
    v_ext = jnp.concatenate([prev_a[2 + reach :], values, next_a[reach + 2 : reach + 4]], axis=0)
    g_ext = jnp.concatenate([cotangent, next_a[reach + 4 :]], axis=0)

    q_short = fwd_short(q_ext, w_q)
    k_short = fwd_short(k_ext, w_k)
    v_first = fwd_short(v_ext, w_v)
    u_first = (k_short * v_first).astype(jnp.bfloat16)
    gz_last = (g_ext.astype(jnp.float32) * q_short).astype(jnp.bfloat16)

    sig_a = jnp.where(first, u_first, gz_last)
    conv_a = depthwise(sig_a, jnp.where(first, back, taps)) + skip_row * jnp.where(
        first, u_first[extent - 1 :], gz_last[: rows + 2]
    ).astype(jnp.float32)
    out_first = (q_short[:rows] * conv_a[:rows]).astype(jnp.bfloat16)
    gvs_last = (conv_a * k_short[extent - 1 :]).astype(jnp.bfloat16)
    gin_last = bwd_short(gvs_last, w_v).astype(jnp.bfloat16)

    handed = lax.ppermute(jnp.where(first, out_first, gin_last), "section", [(0, 1), (1, 0)])
    prev_b = from_prev(handed[-reach:])
    next_b = from_next(handed[:reach])
    y_ext = jnp.concatenate([prev_b, handed, next_b], axis=0)

    gz_first = (y_ext[reach:].astype(jnp.float32) * q_short).astype(jnp.bfloat16)
    v_last = fwd_short(y_ext[: reach + rows + 2], w_v)
    u_last = (k_short * v_last).astype(jnp.bfloat16)
    sig_b = jnp.where(first, gz_first, u_last)
    conv_b = depthwise(sig_b, jnp.where(first, taps, back)) + skip_row * jnp.where(
        first, gz_first[: rows + 2], u_last[extent - 1 :]
    ).astype(jnp.float32)

    z = jnp.where(first, conv_a, conv_b)
    gu = jnp.where(first, conv_b, conv_a)
    v_short = jnp.where(first, v_first, v_last)
    u = jnp.where(first, u_first, u_last)
    g = jnp.where(first, y_ext[reach : reach + rows + 2], g_ext[: rows + 2]).astype(jnp.float32)
    gz = jnp.where(first, gz_first, gz_last)

    output = (q_short[:rows] * z[:rows]).astype(jnp.bfloat16)
    gqs = (g * z).astype(jnp.bfloat16)
    gks = (gu * v_short[extent - 1 :]).astype(jnp.bfloat16)
    gvs = (gu * k_short[extent - 1 :]).astype(jnp.bfloat16)
    grad_q = bwd_short(gqs, w_q).astype(jnp.bfloat16)
    grad_k = bwd_short(gks, w_k).astype(jnp.bfloat16)
    grad_input = bwd_short(gvs, w_v).astype(jnp.bfloat16)
    taps_part = depthwise(u[: rows + extent - 1], gz[:rows])[::-1]
    tap_sum = exchange_scatter(taps_part, "ctx")
    return (output[None], grad_q[None], grad_k[None], grad_input[None], tap_sum[None])


def solution(mesh):
    return jax.shard_map(
        body,
        mesh=mesh,
        in_specs=(
            P("section", "ctx", "chan"),
            P("section", "ctx", "chan"),
            P("ctx", "chan"),
            P("ctx", "chan"),
            P("section", None, None, "chan"),
            P("section", None, "chan"),
            P("section", "chan"),
        ),
        out_specs=(
            P("section", "ctx", "chan"),
            P("section", "ctx", "chan"),
            P("section", "ctx", "chan"),
            P("section", "ctx", "chan"),
            P("section", "ctx", "chan"),
        ),
        check_vma=False,
    )
```

```python
import jax
import jax.numpy as jnp
from jax import lax
from jax.sharding import PartitionSpec as P


def shifted(value, axis, by):
    peers = lax.axis_size(axis)
    pairs = [(i, i + by) for i in range(peers) if 0 <= i + by < peers]
    return lax.ppermute(value, axis, pairs)


def halving_scatter(part, axis):
    peers = lax.axis_size(axis)
    steps = peers.bit_length() - 1
    if peers != 1 << steps or part.shape[0] % peers:
        return lax.psum_scatter(part, axis, scatter_dimension=0, tiled=True)
    me = lax.axis_index(axis)
    rows = part.shape[0] // peers
    held = part.reshape((2,) * steps + (rows,) + part.shape[1:])
    remaining = [steps - 1 - k for k in range(steps)]
    order = [0, 2, 1, 3, 4] if steps == 5 else list(range(steps))
    for bit in order:
        at = remaining.index(bit)
        mine = (me >> bit) & 1
        keep = lax.dynamic_index_in_dim(held, mine, axis=at, keepdims=False)
        give = lax.dynamic_index_in_dim(held, 1 - mine, axis=at, keepdims=False)
        got = lax.ppermute(give, axis, [(i, i ^ (1 << bit)) for i in range(peers)])
        held = keep + got
        remaining.pop(at)
    return held.reshape((rows,) + part.shape[1:])


def exchange_scatter(part, axis):
    peers = lax.axis_size(axis)
    if part.shape[0] % peers:
        return lax.psum_scatter(part[::-1], axis, scatter_dimension=0, tiled=True)
    rows = part.shape[0] // peers
    pieces = part.reshape((peers, rows) + part.shape[1:])[::-1]
    got = lax.all_to_all(pieces.astype(jnp.bfloat16), axis, 0, 0)
    return jnp.sum(got.astype(jnp.float32), axis=0)[::-1]


def depthwise(source, kernel):
    result = lax.conv_general_dilated(
        source[None],
        kernel[:, None, :],
        (1,),
        "VALID",
        dimension_numbers=("NWC", "WIO", "NWC"),
        feature_group_count=source.shape[1],
        preferred_element_type=jnp.float32,
    )
    return result[0]


def fwd_short(rows, weights):
    wide = rows.astype(jnp.float32)
    return weights[0] * wide[2:] + weights[1] * wide[1:-1] + weights[2] * wide[:-2]


def bwd_short(rows, weights):
    wide = rows.astype(jnp.float32)
    return weights[0] * wide[:-2] + weights[1] * wide[1:-1] + weights[2] * wide[2:]


def from_prev(value):
    return shifted(value, "ctx", 1)


def from_next(value):
    return shifted(value, "ctx", -1)


def body(queries, keys, values, cotangent, short_filter, mix_filter, skip):
    first = lax.axis_index("section") == 0
    q, k = queries[0], keys[0]
    w_q, w_k, w_v = short_filter[0][0], short_filter[0][1], short_filter[0][2]
    taps = mix_filter[0]
    extent = taps.shape[0]
    back = taps[::-1]
    skip_row = skip[0]
    rows = q.shape[0]
    reach = extent + 1

    prev_a = from_prev(jnp.concatenate([q[-2:], k[-reach:], values[-reach:]], axis=0))
    next_a = from_next(jnp.concatenate([q[:reach], k[:2], values[:2], cotangent[:reach]], axis=0))
    q_ext = jnp.concatenate([prev_a[:2], q, next_a[:reach]], axis=0)
    k_ext = jnp.concatenate([prev_a[2 : 2 + reach], k, next_a[reach : reach + 2]], axis=0)
    v_ext = jnp.concatenate([prev_a[2 + reach :], values, next_a[reach + 2 : reach + 4]], axis=0)
    g_ext = jnp.concatenate([cotangent, next_a[reach + 4 :]], axis=0)

    q_short = fwd_short(q_ext, w_q)
    k_short = fwd_short(k_ext, w_k)
    v_first = fwd_short(v_ext, w_v)
    u_first = (k_short * v_first).astype(jnp.bfloat16)
    gz_last = (g_ext.astype(jnp.float32) * q_short).astype(jnp.bfloat16)

    sig_a = jnp.where(first, u_first, gz_last)
    conv_a = depthwise(sig_a, jnp.where(first, back, taps)) + skip_row * jnp.where(
        first, u_first[extent - 1 :], gz_last[: rows + 2]
    ).astype(jnp.float32)
    out_first = (q_short[:rows] * conv_a[:rows]).astype(jnp.bfloat16)
    gvs_last = (conv_a * k_short[extent - 1 :]).astype(jnp.bfloat16)
    gin_last = bwd_short(gvs_last, w_v).astype(jnp.bfloat16)

    handed = lax.ppermute(jnp.where(first, out_first, gin_last), "section", [(0, 1), (1, 0)])
    prev_b = from_prev(handed[-reach:])
    next_b = from_next(handed[:reach])
    y_ext = jnp.concatenate([prev_b, handed, next_b], axis=0)

    gz_first = (y_ext[reach:].astype(jnp.float32) * q_short).astype(jnp.bfloat16)
    v_last = fwd_short(y_ext[: reach + rows + 2], w_v)
    u_last = (k_short * v_last).astype(jnp.bfloat16)
    sig_b = jnp.where(first, gz_first, u_last)
    conv_b = depthwise(sig_b, jnp.where(first, taps, back)) + skip_row * jnp.where(
        first, gz_first[: rows + 2], u_last[extent - 1 :]
    ).astype(jnp.float32)

    z = jnp.where(first, conv_a, conv_b)
    gu = jnp.where(first, conv_b, conv_a)
    v_short = jnp.where(first, v_first, v_last)
    u = jnp.where(first, u_first, u_last)
    g = jnp.where(first, y_ext[reach : reach + rows + 2], g_ext[: rows + 2]).astype(jnp.float32)
    gz = jnp.where(first, gz_first, gz_last)

    output = (q_short[:rows] * z[:rows]).astype(jnp.bfloat16)
    gqs = (g * z).astype(jnp.bfloat16)
    gks = (gu * v_short[extent - 1 :]).astype(jnp.bfloat16)
    gvs = (gu * k_short[extent - 1 :]).astype(jnp.bfloat16)
    grad_q = bwd_short(gqs, w_q).astype(jnp.bfloat16)
    grad_k = bwd_short(gks, w_k).astype(jnp.bfloat16)
    grad_input = bwd_short(gvs, w_v).astype(jnp.bfloat16)
    lags = depthwise(u[: rows + extent - 1], gz[:rows])
    tap_sum = exchange_scatter(lags, "ctx")
    return (output[None], grad_q[None], grad_k[None], grad_input[None], tap_sum[None])


def solution(mesh):
    return jax.shard_map(
        body,
        mesh=mesh,
        in_specs=(
            P("section", "ctx", "chan"),
            P("section", "ctx", "chan"),
            P("ctx", "chan"),
            P("ctx", "chan"),
            P("section", None, None, "chan"),
            P("section", None, "chan"),
            P("section", "chan"),
        ),
        out_specs=(
            P("section", "ctx", "chan"),
            P("section", "ctx", "chan"),
            P("section", "ctx", "chan"),
            P("section", "ctx", "chan"),
            P("section", "ctx", "chan"),
        ),
        check_vma=False,
    )
```

```python
import jax
import jax.numpy as jnp
from jax import lax
from jax.sharding import PartitionSpec as P


def shifted(value, axis, by):
    peers = lax.axis_size(axis)
    pairs = [(i, i + by) for i in range(peers) if 0 <= i + by < peers]
    return lax.ppermute(value, axis, pairs)


def halving_scatter(part, axis):
    peers = lax.axis_size(axis)
    steps = peers.bit_length() - 1
    if peers != 1 << steps or part.shape[0] % peers:
        return lax.psum_scatter(part, axis, scatter_dimension=0, tiled=True)
    me = lax.axis_index(axis)
    rows = part.shape[0] // peers
    held = part.reshape((2,) * steps + (rows,) + part.shape[1:])
    remaining = [steps - 1 - k for k in range(steps)]
    order = [0, 2, 1, 3, 4] if steps == 5 else list(range(steps))
    for bit in order:
        at = remaining.index(bit)
        mine = (me >> bit) & 1
        keep = lax.dynamic_index_in_dim(held, mine, axis=at, keepdims=False)
        give = lax.dynamic_index_in_dim(held, 1 - mine, axis=at, keepdims=False)
        got = lax.ppermute(give, axis, [(i, i ^ (1 << bit)) for i in range(peers)])
        held = keep + got
        remaining.pop(at)
    return held.reshape((rows,) + part.shape[1:])


def exchange_scatter(part, axis):
    peers = lax.axis_size(axis)
    if part.shape[0] % peers:
        return lax.psum_scatter(part, axis, scatter_dimension=0, tiled=True)
    rows = part.shape[0] // peers
    pieces = part.reshape((peers, rows) + part.shape[1:])
    got = lax.all_to_all(pieces.astype(jnp.bfloat16), axis, 0, 0)
    return jnp.sum(got.astype(jnp.float32), axis=0)


def depthwise(source, kernel):
    result = lax.conv_general_dilated(
        source[None],
        kernel[:, None, :],
        (1,),
        "VALID",
        dimension_numbers=("NWC", "WIO", "NWC"),
        feature_group_count=source.shape[1],
        preferred_element_type=jnp.float32,
    )
    return result[0]


def fwd_short(rows, weights):
    wide = rows.astype(jnp.float32)
    return weights[0] * wide[2:] + weights[1] * wide[1:-1] + weights[2] * wide[:-2]


def bwd_short(rows, weights):
    wide = rows.astype(jnp.float32)
    return weights[0] * wide[:-2] + weights[1] * wide[1:-1] + weights[2] * wide[2:]


def from_prev(value):
    return shifted(value, "ctx", 1)


def from_next(value):
    return shifted(value, "ctx", -1)


def body(queries, keys, values, cotangent, short_filter, mix_filter, skip):
    first = lax.axis_index("section") == 0
    q, k = queries[0], keys[0]
    w_q, w_k, w_v = short_filter[0][0], short_filter[0][1], short_filter[0][2]
    taps = mix_filter[0]
    extent = taps.shape[0]
    back = taps[::-1]
    skip_row = skip[0]
    rows = q.shape[0]
    reach = extent + 1

    peers = lax.axis_size("ctx")
    both = ("section", "ctx")
    down = [(i, i + 1) for i in range(peers - 1)]
    up = [(i + 1, i) for i in range(peers - 1)]
    late = lambda pairs: [(peers + a, peers + b) for a, b in pairs]
    pad = jnp.zeros((2,) + q.shape[1:], q.dtype)
    wide = lax.ppermute(
        jnp.where(
            first,
            jnp.concatenate([q[-2:], k[-reach:], values[-reach:]], axis=0),
            jnp.concatenate([q[:reach], cotangent[:reach], k[:2]], axis=0),
        ),
        both,
        down + late(up),
    )
    narrow = lax.ppermute(
        jnp.where(
            first,
            jnp.concatenate([q[:reach], k[:2], values[:2]], axis=0),
            jnp.concatenate([q[-2:], k[-reach:], pad], axis=0),
        ),
        both,
        up + late(down),
    )
    q_ext = jnp.concatenate(
        [jnp.where(first, wide[:2], narrow[:2]), q, jnp.where(first, narrow[:reach], wide[:reach])],
        axis=0,
    )
    k_ext = jnp.concatenate(
        [
            jnp.where(first, wide[2 : 2 + reach], narrow[2 : 2 + reach]),
            k,
            jnp.where(first, narrow[reach : reach + 2], wide[2 * reach :]),
        ],
        axis=0,
    )
    v_ext = jnp.concatenate([wide[2 + reach :], values, narrow[reach + 2 :]], axis=0)
    g_ext = jnp.concatenate([cotangent, wide[reach : 2 * reach]], axis=0)

    q_short = fwd_short(q_ext, w_q)
    k_short = fwd_short(k_ext, w_k)
    v_first = fwd_short(v_ext, w_v)
    u_first = (k_short * v_first).astype(jnp.bfloat16)
    gz_last = (g_ext.astype(jnp.float32) * q_short).astype(jnp.bfloat16)

    sig_a = jnp.where(first, u_first, gz_last)
    conv_a = depthwise(sig_a, jnp.where(first, back, taps)) + skip_row * jnp.where(
        first, u_first[extent - 1 :], gz_last[: rows + 2]
    ).astype(jnp.float32)
    out_first = (q_short[:rows] * conv_a[:rows]).astype(jnp.bfloat16)
    gvs_last = (conv_a * k_short[extent - 1 :]).astype(jnp.bfloat16)
    gin_last = bwd_short(gvs_last, w_v).astype(jnp.bfloat16)

    handed = lax.ppermute(jnp.where(first, out_first, gin_last), "section", [(0, 1), (1, 0)])
    rim = lax.ppermute(jnp.where(first, handed[:reach], handed[-reach:]), both, up + late(down))
    ahead = lax.ppermute(handed[:2], both, late(up))
    y_ext = jnp.concatenate(
        [rim, handed, jnp.where(first, rim[:2], ahead), rim[2:]], axis=0
    )

    gz_first = (y_ext[reach:].astype(jnp.float32) * q_short).astype(jnp.bfloat16)
    v_last = fwd_short(y_ext[: reach + rows + 2], w_v)
    u_last = (k_short * v_last).astype(jnp.bfloat16)
    sig_b = jnp.where(first, gz_first, u_last)
    conv_b = depthwise(sig_b, jnp.where(first, taps, back)) + skip_row * jnp.where(
        first, gz_first[: rows + 2], u_last[extent - 1 :]
    ).astype(jnp.float32)

    z = jnp.where(first, conv_a, conv_b)
    gu = jnp.where(first, conv_b, conv_a)
    v_short = jnp.where(first, v_first, v_last)
    u = jnp.where(first, u_first, u_last)
    g = jnp.where(first, y_ext[reach : reach + rows + 2], g_ext[: rows + 2]).astype(jnp.float32)
    gz = jnp.where(first, gz_first, gz_last)

    output = (q_short[:rows] * z[:rows]).astype(jnp.bfloat16)
    gqs = (g * z).astype(jnp.bfloat16)
    gks = (gu * v_short[extent - 1 :]).astype(jnp.bfloat16)
    gvs = (gu * k_short[extent - 1 :]).astype(jnp.bfloat16)
    grad_q = bwd_short(gqs, w_q).astype(jnp.bfloat16)
    grad_k = bwd_short(gks, w_k).astype(jnp.bfloat16)
    grad_input = bwd_short(gvs, w_v).astype(jnp.bfloat16)
    taps_part = depthwise(u[: rows + extent - 1], gz[:rows])[::-1]
    tap_sum = exchange_scatter(taps_part, "ctx")
    return (output[None], grad_q[None], grad_k[None], grad_input[None], tap_sum[None])


def solution(mesh):
    return jax.shard_map(
        body,
        mesh=mesh,
        in_specs=(
            P("section", "ctx", "chan"),
            P("section", "ctx", "chan"),
            P("ctx", "chan"),
            P("ctx", "chan"),
            P("section", None, None, "chan"),
            P("section", None, "chan"),
            P("section", "chan"),
        ),
        out_specs=(
            P("section", "ctx", "chan"),
            P("section", "ctx", "chan"),
            P("section", "ctx", "chan"),
            P("section", "ctx", "chan"),
            P("section", "ctx", "chan"),
        ),
        check_vma=False,
    )
```

```python
import jax
import jax.numpy as jnp
from jax import lax
from jax.sharding import PartitionSpec as P


def shifted(value, axis, by):
    peers = lax.axis_size(axis)
    pairs = [(i, i + by) for i in range(peers) if 0 <= i + by < peers]
    return lax.ppermute(value, axis, pairs)


def halving_scatter(part, axis):
    peers = lax.axis_size(axis)
    steps = peers.bit_length() - 1
    if peers != 1 << steps or part.shape[0] % peers:
        return lax.psum_scatter(part[::-1], axis, scatter_dimension=0, tiled=True)
    me = lax.axis_index(axis)
    rows = part.shape[0] // peers
    held = part.reshape((2,) * steps + (rows,) + part.shape[1:])
    remaining = [steps - 1 - k for k in range(steps)]
    order = [0, 2, 1, 3, 4] if steps == 5 else list(range(steps))
    for bit in order:
        at = remaining.index(bit)
        mine = (me >> bit) & 1
        keep = lax.dynamic_index_in_dim(held, mine, axis=at, keepdims=False)
        give = lax.dynamic_index_in_dim(held, 1 - mine, axis=at, keepdims=False)
        got = lax.ppermute(give, axis, [(i, i ^ (1 << bit)) for i in range(peers)])
        held = keep + got
        remaining.pop(at)
    return held.reshape((rows,) + part.shape[1:])


def exchange_scatter(part, axis):
    peers = lax.axis_size(axis)
    if part.shape[0] % peers:
        return lax.psum_scatter(part[::-1], axis, scatter_dimension=0, tiled=True)
    rows = part.shape[0] // peers
    pieces = part.reshape((peers, rows) + part.shape[1:])[::-1]
    got = lax.all_to_all(pieces.astype(jnp.bfloat16), axis, 0, 0)
    return jnp.sum(got.astype(jnp.float32), axis=0)[::-1]


def depthwise(source, kernel):
    result = lax.conv_general_dilated(
        source[None],
        kernel[:, None, :],
        (1,),
        "VALID",
        dimension_numbers=("NWC", "WIO", "NWC"),
        feature_group_count=source.shape[1],
        preferred_element_type=jnp.float32,
    )
    return result[0]


def fwd_short(rows, weights):
    wide = rows.astype(jnp.float32)
    return weights[0] * wide[2:] + weights[1] * wide[1:-1] + weights[2] * wide[:-2]


def bwd_short(rows, weights):
    wide = rows.astype(jnp.float32)
    return weights[0] * wide[:-2] + weights[1] * wide[1:-1] + weights[2] * wide[2:]


def from_prev(value):
    return shifted(value, "ctx", 1)


def from_next(value):
    return shifted(value, "ctx", -1)


def body(queries, keys, values, cotangent, short_filter, mix_filter, skip):
    first = lax.axis_index("section") == 0
    q, k = queries[0], keys[0]
    w_q, w_k, w_v = short_filter[0][0], short_filter[0][1], short_filter[0][2]
    taps = mix_filter[0]
    extent = taps.shape[0]
    back = taps[::-1]
    skip_row = skip[0]
    rows = q.shape[0]
    reach = extent + 1

    peers = lax.axis_size("ctx")
    both = ("section", "ctx")
    down = [(i, i + 1) for i in range(peers - 1)]
    up = [(i + 1, i) for i in range(peers - 1)]
    late = lambda pairs: [(peers + a, peers + b) for a, b in pairs]
    pad = jnp.zeros((2,) + q.shape[1:], q.dtype)
    wide = lax.ppermute(
        jnp.where(
            first,
            jnp.concatenate([q[-2:], k[-reach:], values[-reach:]], axis=0),
            jnp.concatenate([q[:reach], cotangent[:reach], k[:2]], axis=0),
        ),
        both,
        down + late(up),
    )
    narrow = lax.ppermute(
        jnp.where(
            first,
            jnp.concatenate([q[:reach], k[:2], values[:2]], axis=0),
            jnp.concatenate([q[-2:], k[-reach:], pad], axis=0),
        ),
        both,
        up + late(down),
    )
    q_ext = jnp.concatenate(
        [jnp.where(first, wide[:2], narrow[:2]), q, jnp.where(first, narrow[:reach], wide[:reach])],
        axis=0,
    )
    k_ext = jnp.concatenate(
        [
            jnp.where(first, wide[2 : 2 + reach], narrow[2 : 2 + reach]),
            k,
            jnp.where(first, narrow[reach : reach + 2], wide[2 * reach :]),
        ],
        axis=0,
    )
    v_ext = jnp.concatenate([wide[2 + reach :], values, narrow[reach + 2 :]], axis=0)
    g_ext = jnp.concatenate([cotangent, wide[reach : 2 * reach]], axis=0)

    q_short = fwd_short(q_ext, w_q)
    k_short = fwd_short(k_ext, w_k)
    v_first = fwd_short(v_ext, w_v)
    u_first = (k_short * v_first).astype(jnp.bfloat16)
    gz_last = (g_ext.astype(jnp.float32) * q_short).astype(jnp.bfloat16)

    sig_a = jnp.where(first, u_first, gz_last)
    conv_a = depthwise(sig_a, jnp.where(first, back, taps)) + skip_row * jnp.where(
        first, u_first[extent - 1 :], gz_last[: rows + 2]
    ).astype(jnp.float32)
    out_first = (q_short[:rows] * conv_a[:rows]).astype(jnp.bfloat16)
    gvs_last = (conv_a * k_short[extent - 1 :]).astype(jnp.bfloat16)
    gin_last = bwd_short(gvs_last, w_v).astype(jnp.bfloat16)

    handed = lax.ppermute(jnp.where(first, out_first, gin_last), "section", [(0, 1), (1, 0)])
    rim = lax.ppermute(jnp.where(first, handed[:reach], handed[-reach:]), both, up + late(down))
    ahead = lax.ppermute(handed[:2], both, late(up))
    y_ext = jnp.concatenate(
        [rim, handed, jnp.where(first, rim[:2], ahead), rim[2:]], axis=0
    )

    gz_first = (y_ext[reach:].astype(jnp.float32) * q_short).astype(jnp.bfloat16)
    v_last = fwd_short(y_ext[: reach + rows + 2], w_v)
    u_last = (k_short * v_last).astype(jnp.bfloat16)
    sig_b = jnp.where(first, gz_first, u_last)
    conv_b = depthwise(sig_b, jnp.where(first, taps, back)) + skip_row * jnp.where(
        first, gz_first[: rows + 2], u_last[extent - 1 :]
    ).astype(jnp.float32)

    z = jnp.where(first, conv_a, conv_b)
    gu = jnp.where(first, conv_b, conv_a)
    v_short = jnp.where(first, v_first, v_last)
    u = jnp.where(first, u_first, u_last)
    g = jnp.where(first, y_ext[reach : reach + rows + 2], g_ext[: rows + 2]).astype(jnp.float32)
    gz = jnp.where(first, gz_first, gz_last)

    output = (q_short[:rows] * z[:rows]).astype(jnp.bfloat16)
    gqs = (g * z).astype(jnp.bfloat16)
    gks = (gu * v_short[extent - 1 :]).astype(jnp.bfloat16)
    gvs = (gu * k_short[extent - 1 :]).astype(jnp.bfloat16)
    grad_q = bwd_short(gqs, w_q).astype(jnp.bfloat16)
    grad_k = bwd_short(gks, w_k).astype(jnp.bfloat16)
    grad_input = bwd_short(gvs, w_v).astype(jnp.bfloat16)
    taps_part = depthwise(u[: rows + extent - 1], gz[:rows])
    tap_sum = exchange_scatter(taps_part, "ctx")
    return (output[None], grad_q[None], grad_k[None], grad_input[None], tap_sum[None])


def solution(mesh):
    return jax.shard_map(
        body,
        mesh=mesh,
        in_specs=(
            P("section", "ctx", "chan"),
            P("section", "ctx", "chan"),
            P("ctx", "chan"),
            P("ctx", "chan"),
            P("section", None, None, "chan"),
            P("section", None, "chan"),
            P("section", "chan"),
        ),
        out_specs=(
            P("section", "ctx", "chan"),
            P("section", "ctx", "chan"),
            P("section", "ctx", "chan"),
            P("section", "ctx", "chan"),
            P("section", "ctx", "chan"),
        ),
        check_vma=False,
    )
```
